32 devices in a mesh: tm: 16 (over z, y, core), space: 2 (over x).
Axes of the slice: x: 2, y: 2, z: 4, core: 2. Of those that a mesh axis runs over, the one named last changes fastest.
Arguments:
- u_init: float32 [2, 512, 512], P(None, 'space'), may hold values from -8 to 8
- phase: float32 [512, 512], P('space'), may hold values from 0.005 to 0.05
- absorb: float32 [512, 512], P('space'), may hold values from 0.004 to 0.04
Outputs:
- solution: float32 [2, 16, 512, 512], P(None, 'tm', 'space')
The draws below stay inside these ranges and needn't reach their ends.
All inputs are finite; a program needn't handle non-finite values.
Results may differ from the reference program's by a relative error of at most 0.0003.
Values sent between devices are 32-bit elements; how exact they have to be, the bound alone decides.
A program may use at most 192 MiB of HBM per device.

```python
import math
import jax
import jax.numpy as jnp

NX = 512
NY = 512
ITERS = 4
TIME = 16


def draw_u_init(key, part):
    key_noise = jax.random.fold_in(key, 11)
    noise = jax.random.normal(key_noise, (2, NX, NY), jnp.float32)
    return jnp.clip(noise, -6.0, 6.0)


def block_levels(stream_key, dims, pieces, smallest, top_value):
    factor_of, own = 1.0, jax.random.fold_in(stream_key, 6)
    for axis_at, shards_of in pieces:
        draws = jnp.exp(jax.random.uniform(jax.random.fold_in(own, axis_at), (shards_of,), jnp.float32, smallest / len(pieces), top_value / len(pieces)))
        factor_of = factor_of * jnp.repeat(draws, dims[axis_at] // shards_of).reshape([-1 if axis == axis_at else 1 for axis in range(len(dims))])
    return factor_of


def setup_inputs(seed: int = 0) -> dict:
    arg_keys = jax.random.split(jax.random.key(seed), 4)
    return {
        "u_init": draw_u_init(jax.random.fold_in(arg_keys[3], 71), 0),
        "phase": jnp.clip(jnp.exp(math.log(0.05) - 2.3025851 * jax.random.uniform(arg_keys[1], (NX, NY), jnp.float32) ** block_levels(arg_keys[1], (NX, NY), ((0, 2),), -0.2, 0.2)), 0.005, 0.05),
        "absorb": jnp.clip(jnp.exp(math.log(0.04) - 2.30258502 * jax.random.uniform(arg_keys[2], (NX, NY), jnp.float32) ** block_levels(arg_keys[2], (NX, NY), ((0, 2),), -0.2, 0.2)), 0.004, 0.04),
    }


tau = 400.0
alpha = 0.4

def laplacian(field):
    return jnp.roll(field, 1, -2) + jnp.roll(field, -1, -2) + jnp.roll(field, 1, -1) + jnp.roll(field, -1, -1) - 4.0 * field

def generator(field, phase, absorb):
    curvature = laplacian(field)
    change_real = -tau * curvature[1] + phase * field[1] - absorb * field[0]
    change_imag = tau * curvature[0] - phase * field[0] - absorb * field[1]
    return jnp.stack([change_real, change_imag])

def operate(field, phase, absorb):
    change = generator(field, phase, absorb)
    ahead = field + 0.5 * change
    behind = field - 0.5 * change
    previous = jnp.concatenate([jnp.zeros_like(ahead[:, :1]), ahead[:, :-1]], axis=1)
    return behind - previous

def precondition(field, weights, ratio_real, ratio_imag):
    weighted = field * weights[None, :, None, None]
    spectrum = jnp.fft.fftn(weighted[0] + 1j * weighted[1], axes=(0, 1, 2))
    solved = spectrum * (ratio_real - 1j * ratio_imag)
    back = jnp.fft.ifftn(solved, axes=(0, 1, 2))
    result = jnp.stack([jnp.real(back), jnp.imag(back)]).astype(jnp.float32)
    return result / weights[None, :, None, None]

def least_squares(hessenberg, start):
    matrix = [list(line) for line in hessenberg]
    target = [start] + [jnp.zeros((), jnp.float32) for unused in range(ITERS)]
    cosines = []
    sines = []
    for column in range(ITERS):
        for row in range(column):
            upper = matrix[row][column]
            lower = matrix[row + 1][column]
            matrix[row][column] = cosines[row] * upper + sines[row] * lower
            matrix[row + 1][column] = -sines[row] * upper + cosines[row] * lower
        upper = matrix[column][column]
        lower = matrix[column + 1][column]
        radius = jnp.sqrt(upper * upper + lower * lower)
        cosines.append(upper / radius)
        sines.append(lower / radius)
        matrix[column][column] = radius
        target[column + 1] = -sines[column] * target[column]
        target[column] = cosines[column] * target[column]
    factors = [None] * ITERS
    for row in reversed(range(ITERS)):
        total = target[row]
        for other in range(row + 1, ITERS):
            total = total - matrix[row][other] * factors[other]
        factors[row] = total / matrix[row][row]
    return factors

def reference(u_init, phase, absorb):
    beta = jnp.float32(alpha) ** (1.0 / TIME)
    steps = jnp.arange(TIME).astype(jnp.float32)
    weights = jnp.float32(alpha) ** (steps / TIME)
    theta = steps * (2.0 * math.pi / TIME)
    cosine = (beta * jnp.cos(theta))[:, None, None]
    sine = (beta * jnp.sin(theta))[:, None, None]
    symbol_x = 4.0 * jnp.sin(jnp.arange(NX).astype(jnp.float32) * (math.pi / NX)) ** 2
    symbol_y = 4.0 * jnp.sin(jnp.arange(NY).astype(jnp.float32) * (math.pi / NY)) ** 2
    symbol = (symbol_x[:, None] + symbol_y[None, :])[None]
    eigen_real = 1.0 - cosine + tau * symbol * sine / 2.0
    eigen_imag = sine + tau * symbol * (1.0 + cosine) / 2.0
    modulus = eigen_real * eigen_real + eigen_imag * eigen_imag
    ratio_real = eigen_real / modulus
    ratio_imag = eigen_imag / modulus
    first = u_init + 0.5 * generator(u_init, phase, absorb)
    right_side = jnp.concatenate([first[:, None], jnp.zeros((2, TIME - 1, NX, NY), jnp.float32)], axis=1)
    start = jnp.sqrt(jnp.sum(right_side * right_side))
    basis = [right_side / start]
    corrected = []
    hessenberg = [[jnp.zeros((), jnp.float32) for unused in range(ITERS)] for other in range(ITERS + 1)]
    for column in range(ITERS):
        update = precondition(basis[column], weights, ratio_real, ratio_imag)
        corrected.append(update)
        image = operate(update, phase, absorb)
        products = [jnp.sum(image * vector) for vector in basis]
        for vector, amount in zip(basis, products):
            image = image - amount * vector
        length = jnp.sqrt(jnp.sum(image * image))
        for row in range(column + 1):
            hessenberg[row][column] = products[row]
        hessenberg[column + 1][column] = length
        if column + 1 < ITERS:
            basis.append(image / length)
    factors = least_squares(hessenberg, start)
    solution = jnp.zeros((2, TIME, NX, NY), jnp.float32)
    for amount, update in zip(factors, corrected):
        solution = solution + amount * update
    return solution
```

```python
import functools
import math

import jax
import jax.numpy as jnp
import numpy as np
from jax import lax
from jax.experimental import pallas as pl
from jax.experimental.pallas import tpu as pltpu
from jax.sharding import PartitionSpec as P

ITERS = 4
tau = 400.0
alpha = 0.4
theta = alpha / (1.0 - alpha)
highest = lax.Precision.HIGHEST
AXES = ("tm", "space")
vmem = pl.BlockSpec(memory_space=pltpu.VMEM)


def with_halo(cells, axis, dim):
    count = lax.axis_size(axis)
    head = lax.slice_in_dim(cells, 0, 1, axis=dim)
    tail = lax.slice_in_dim(cells, cells.shape[dim] - 1, cells.shape[dim], axis=dim)
    return jnp.concatenate(
        [
            lax.ppermute(tail, axis, [(i, (i + 1) % count) for i in range(count)]),
            cells,
            lax.ppermute(head, axis, [((i + 1) % count, i) for i in range(count)]),
        ],
        axis=dim,
    )


def first_side(field, phase, absorb):
    padded = with_halo(field, "space", 1)
    curvature = (
        padded[:, 2:] + padded[:, :-2] + jnp.roll(field, 1, 2) + jnp.roll(field, -1, 2) - 4.0 * field
    )
    change_real = -tau * curvature[1] + phase * field[1] - absorb * field[0]
    change_imag = tau * curvature[0] - phase * field[0] - absorb * field[1]
    return field + 0.5 * jnp.stack([change_real, change_imag])


def tables(length):
    index = np.arange(length)
    angle = (index[:, None] * index[None, :] % length) * (2.0 * math.pi / length)
    return np.cos(angle).astype(np.float32), np.sin(angle).astype(np.float32)


def halves(value):
    high = value.astype(jnp.bfloat16)
    return high, (value - high.astype(jnp.float32)).astype(jnp.bfloat16)


def product(left, right):
    dot = functools.partial(jnp.dot, preferred_element_type=jnp.float32)
    return dot(left[0], right[0]) + (dot(left[0], right[1]) + dot(left[1], right[0]))


def split_kernel(cos_ref, sin_ref, ch_ref, cl_ref, sh_ref, sl_ref):
    ch_ref[...], cl_ref[...] = halves(cos_ref[...])
    sh_ref[...], sl_ref[...] = halves(sin_ref[...])


def grid_kernel(
    steps, got_ref, ch_ref, cl_ref, sh_ref, sl_ref, lc_ref, ls_ref, phase_ref, absorb_ref, z_ref, out_ref
):
    devices, _, block, lanes = got_ref.shape
    size = devices * block
    cosine = (ch_ref[...], cl_ref[...])
    sine = (sh_ref[...], sl_ref[...])
    real = halves(got_ref[:, 0].reshape(size, lanes))
    imag = halves(got_ref[:, 1].reshape(size, lanes))
    mid_real = halves(product(cosine, real) - product(sine, imag))
    mid_imag = halves(product(sine, real) + product(cosine, imag))
    lane_cos, lane_sin = halves(lc_ref[0]), halves(ls_ref[0])
    back_cos, back_sin = halves(lc_ref[1]), halves(ls_ref[1])
    z_real = product(mid_real, back_cos) - product(mid_imag, back_sin)
    z_imag = product(mid_real, back_sin) + product(mid_imag, back_cos)
    z_ref[0] = z_real
    z_ref[1] = z_imag
    late = lax.broadcasted_iota(jnp.int32, (size, lanes), 1) % steps > 0
    sum_real = z_real + jnp.where(late, pltpu.roll(z_real, 1, 1), 0.0)
    sum_imag = z_imag + jnp.where(late, pltpu.roll(z_imag, 1, 1), 0.0)
    phase, absorb = phase_ref[...], absorb_ref[...]
    real = halves(absorb * sum_real - phase * sum_imag)
    imag = halves(absorb * sum_imag + phase * sum_real)
    mid_real = halves(product(real, lane_cos) + product(imag, lane_sin))
    mid_imag = halves(product(imag, lane_cos) - product(real, lane_sin))
    out_ref[:, 0] = (product(cosine, mid_real) + product(sine, mid_imag)).reshape(devices, block, lanes)
    out_ref[:, 1] = (product(cosine, mid_imag) - product(sine, mid_real)).reshape(devices, block, lanes)


def fourier(values, sign):
    count = len(values)
    if count == 1:
        return values
    even = fourier(values[0::2], sign)
    odd = fourier(values[1::2], sign)
    first, second = [], []
    for k in range(count // 2):
        angle = sign * 2.0 * math.pi * k / count
        cosine, sine = math.cos(angle), math.sin(angle)
        real, imag = odd[k]
        if k == 0:
            turned = (real, imag)
        elif 4 * k == count:
            turned = (-imag, real) if sign > 0 else (imag, -real)
        else:
            turned = (cosine * real - sine * imag, cosine * imag + sine * real)
        first.append((even[k][0] + turned[0], even[k][1] + turned[1]))
        second.append((even[k][0] - turned[0], even[k][1] - turned[1]))
    return first + second


def tile_of(block, lanes):
    return min(8, block), min(128, lanes)


def solve_tile(w, coefs, steps, row, lane):
    ratio_real, ratio_imag, scale_real, scale_imag, q = coefs
    wr, wi = w
    zr = wr * scale_real - wi * scale_imag
    zi = wr * scale_imag + wi * scale_real
    width = zr.shape[1]
    when = lax.broadcasted_iota(jnp.int32, zr.shape, 1) % steps

    def wrapped(value, amount):
        back = (amount - steps) % width
        return alpha * (pltpu.roll(value, back, 1) if back else value)

    pr, pi = ratio_real, ratio_imag
    amount = 1
    while amount < steps:
        late = when >= amount
        hr = jnp.where(late, pltpu.roll(zr, amount, 1), wrapped(zr, amount))
        hi = jnp.where(late, pltpu.roll(zi, amount, 1), wrapped(zi, amount))
        zr, zi = zr + pr * hr - pi * hi, zi + pr * hi + pi * hr
        pr, pi = pr * pr - pi * pi, 2.0 * pr * pi
        amount *= 2
    hr, hi = wrapped(zr, 1), wrapped(zi, 1)
    first = when == 0
    xr = jnp.where(first, hr + q * hi, 0.0)
    xi = jnp.where(first, hi - q * hr, 0.0)
    return (zr, zi), (xr - theta * wr, xi - theta * wi)


def mode_kernel(steps, start, last, *refs):
    refs = list(refs)
    got_ref = refs.pop(0)
    carry_ref = None if start else refs.pop(0)
    if last:
        old_refs = [refs.pop(0) for unused in range(ITERS)]
        gram_ref = refs.pop(0)
        devices, block, lanes = got_ref.shape[0], got_ref.shape[2], got_ref.shape[3]
    else:
        coef_refs = [refs.pop(0) for unused in range(5)]
        w_ref = None if start else refs.pop(0)
        next_ref, send_ref = refs
        devices, _, block, lanes = send_ref.shape
    high, wide = tile_of(block, lanes)
    across = lanes // wide
    if last:
        gram_ref[...] = jnp.zeros_like(gram_ref)

    def tile(index, unused):
        row = pl.ds(pl.multiple_of(index // across * high, high), high)
        lane = pl.ds(pl.multiple_of(index % across * wide, wide), wide)
        if start:
            w = [(got_ref[0, k, row, lane], got_ref[1, k, row, lane]) for k in range(devices)]
        else:
            values = [(got_ref[k, 0, row, lane], got_ref[k, 1, row, lane]) for k in range(devices)]
            values = fourier(values, -1)
            w = [
                (values[k][0] + carry_ref[0, k, row, lane], values[k][1] + carry_ref[1, k, row, lane])
                for k in range(devices)
            ]
        if last:
            sums = {}
            for k in range(devices):
                vectors = [(r[0, k, row, lane], r[1, k, row, lane]) for r in old_refs] + [w[k]]
                at = 0
                for i in range(ITERS + 1):
                    for j in range(i + 1):
                        term = vectors[i][0] * vectors[j][0] + vectors[i][1] * vectors[j][1]
                        sums[at] = term if k == 0 else sums[at] + term
                        at += 1
            for at in sums:
                gram_ref[at, 0:high, 0:wide] += sums[at]
            return 0
        solved = []
        for k in range(devices):
            coefs = [ref[k, row, lane] for ref in coef_refs]
            z, carry = solve_tile(w[k], coefs, steps, row, lane)
            if w_ref is not None:
                w_ref[0, k, row, lane] = w[k][0]
                w_ref[1, k, row, lane] = w[k][1]
            next_ref[0, k, row, lane] = carry[0]
            next_ref[1, k, row, lane] = carry[1]
            solved.append(z)
        solved = fourier(solved, 1)
        for k in range(devices):
            send_ref[k, 0, row, lane] = solved[k][0]
            send_ref[k, 1, row, lane] = solved[k][1]
        return 0

    lax.fori_loop(0, (block // high) * across, tile, 0)


def call(kernel, shapes, *args):
    out = [jax.ShapeDtypeStruct(shape, kind) for shape, kind in shapes]
    return pl.pallas_call(
        kernel,
        out_shape=out,
        in_specs=[vmem] * len(args),
        out_specs=[vmem] * len(out),
        compiler_params=pltpu.CompilerParams(vmem_limit_bytes=60 * 1024 * 1024),
    )(*args)


def least_squares(hessenberg, start):
    matrix = [list(line) for line in hessenberg]
    target = [start] + [jnp.zeros((), jnp.float32) for unused in range(ITERS)]
    cosines = []
    sines = []
    for column in range(ITERS):
        for row in range(column):
            upper = matrix[row][column]
            lower = matrix[row + 1][column]
            matrix[row][column] = cosines[row] * upper + sines[row] * lower
            matrix[row + 1][column] = -sines[row] * upper + cosines[row] * lower
        upper = matrix[column][column]
        lower = matrix[column + 1][column]
        radius = jnp.sqrt(upper * upper + lower * lower)
        cosines.append(upper / radius)
        sines.append(lower / radius)
        matrix[column][column] = radius
        target[column + 1] = -sines[column] * target[column]
        target[column] = cosines[column] * target[column]
    factors = [None] * ITERS
    for row in reversed(range(ITERS)):
        total = target[row]
        for other in range(row + 1, ITERS):
            total = total - matrix[row][other] * factors[other]
        factors[row] = total / matrix[row][row]
    return factors


def combination(gram):
    count = ITERS + 1
    entry = lambda i, j: gram[i * (i + 1) // 2 + j] if i >= j else gram[j * (j + 1) // 2 + i]
    norms = [jnp.sqrt(jnp.maximum(entry(i, i), 1e-30)) for i in range(count)]
    factor = [[None] * count for unused in range(count)]
    for j in range(count):
        for i in range(j, count):
            value = entry(i, j) / (norms[i] * norms[j])
            for k in range(j):
                value = value - factor[i][k] * factor[j][k]
            if i == j:
                factor[i][i] = jnp.sqrt(jnp.maximum(value, 1e-10))
            else:
                factor[i][j] = value / factor[j][j]
    zero = jnp.zeros((), jnp.float32)
    upper = [[factor[j][i] * norms[j] if j >= i else zero for j in range(count)] for i in range(count)]
    matrix = [
        [(1.0 + theta) * upper[i][j] + upper[i][j + 1] for j in range(ITERS)] for i in range(count)
    ]
    return least_squares(matrix, norms[0] * factor[0][0])


def exchange(value):
    return lax.all_to_all(value, AXES, split_axis=0, concat_axis=0, tiled=True)


def shards(u_init, phase, absorb):
    steps, spaces = lax.axis_size("tm"), lax.axis_size("space")
    devices = steps * spaces
    columns = u_init.shape[2]
    rows = u_init.shape[1] * spaces
    block = columns // devices
    local = rows // devices
    lanes = local * steps
    inner = local // spaces
    f32 = jnp.float32
    me = lax.axis_index("tm") * spaces + lax.axis_index("space")
    cosine_np, sine_np = tables(columns)
    cosine, sine = jnp.asarray(cosine_np), jnp.asarray(sine_np)
    row_cos_np, row_sin_np = tables(rows)
    half = ((columns, columns), jnp.bfloat16)
    table = call(split_kernel, [half] * 4, cosine, sine)

    first = first_side(u_init, phase, absorb)
    pieces = jnp.concatenate([phase[None], absorb[None]]).reshape(2, inner, devices, columns)
    pieces = lax.dynamic_slice_in_dim(pieces, lax.axis_index("tm") * spaces, spaces, axis=2)
    pieces = lax.all_to_all(pieces, "space", split_axis=2, concat_axis=1, tiled=True)
    pieces = pieces.reshape(2, local, columns)
    spread = np.repeat(np.eye(local, dtype=np.float32), steps, axis=1)
    scale = 0.5 / (rows * columns)
    wide_pieces = jnp.einsum("frq,rl->fql", pieces * scale, jnp.asarray(spread), precision=highest)

    mine = lax.axis_index("tm") * spaces * block
    need_cos = lax.dynamic_slice_in_dim(cosine, mine, spaces * block, axis=0)
    need_sin = lax.dynamic_slice_in_dim(sine, mine, spaces * block, axis=0)
    dot = functools.partial(jnp.einsum, precision=highest)
    column = jnp.stack(
        [
            dot("kq,pq->kp", need_cos, first[0]) + dot("kq,pq->kp", need_sin, first[1]),
            dot("kq,pq->kp", need_cos, first[1]) - dot("kq,pq->kp", need_sin, first[0]),
        ]
    )
    column = lax.all_to_all(column, "space", split_axis=1, concat_axis=2, tiled=True)
    row_cos, row_sin = jnp.asarray(row_cos_np), jnp.asarray(row_sin_np)
    side = jnp.stack(
        [
            dot("kp,pa->ka", column[0], row_cos) + dot("kp,pa->ka", column[1], row_sin),
            dot("kp,pa->ka", column[1], row_cos) - dot("kp,pa->ka", column[0], row_sin),
        ]
    )
    side = side.reshape(2, block, devices, local).transpose(0, 2, 1, 3)
    place = np.zeros((local, lanes), np.float32)
    place[np.arange(local), np.arange(local) * steps] = 1.0
    w = jnp.einsum("cmkr,rl->cmkl", side, jnp.asarray(place), precision=highest)

    lane_index = jnp.arange(lanes) // steps
    mode_x = (lane_index[None, :] + local * jnp.arange(devices)[:, None]).astype(f32)
    mode_y = (me * block + jnp.arange(block)).astype(f32)
    symbol_x = 4.0 * jnp.sin(mode_x * (math.pi / rows)) ** 2
    symbol_y = 4.0 * jnp.sin(mode_y * (math.pi / columns)) ** 2
    q = 0.5 * tau * (symbol_x[:, None, :] + symbol_y[None, :, None])
    below = 1.0 / (1.0 + q * q)
    ratio_real, ratio_imag = (1.0 - q * q) * below, -2.0 * q * below
    pr, pi = ratio_real, ratio_imag
    amount = 1
    while amount < steps:
        pr, pi = pr * pr - pi * pi, 2.0 * pr * pi
        amount *= 2
    dr, di = 1.0 - alpha * pr, -alpha * pi
    dr, di = dr - q * di, di + q * dr
    under = 1.0 / (dr * dr + di * di)
    coefs = (ratio_real, ratio_imag, dr * under, -di * under, q)

    place_of = jnp.arange(lanes)
    at, when = place_of // steps, place_of % steps
    same = (when[:, None] == when[None, :]).astype(f32)
    angle = (at[None, :] * (me + devices * at[:, None])) % rows
    angle = angle.astype(f32) * (2.0 * math.pi / rows)
    lane_cos, lane_sin = jnp.cos(angle) * same, jnp.sin(angle) * same
    lane_cos = jnp.stack([lane_cos, lane_cos.T])
    lane_sin = jnp.stack([lane_sin, lane_sin.T])

    sent = ((devices, 2, block, lanes), f32)
    kept = ((2, devices, block, lanes), f32)
    field = ((2, columns, lanes), f32)
    carry, send = call(functools.partial(mode_kernel, steps, True, False), [kept, sent], w, *coefs)
    basis, updates = [w], []
    for step in range(ITERS):
        z, out = call(
            functools.partial(grid_kernel, steps),
            [field, sent],
            exchange(send),
            *table,
            lane_cos,
            lane_sin,
            wide_pieces[0],
            wide_pieces[1],
        )
        updates.append(z)
        got = exchange(out)
        if step + 1 < ITERS:
            w, carry, send = call(
                functools.partial(mode_kernel, steps, False, False), [kept, kept, sent], got, carry, *coefs
            )
            basis.append(w)
    pairs = (ITERS + 1) * (ITERS + 2) // 2
    (gram,) = call(
        functools.partial(mode_kernel, steps, False, True),
        [((pairs, 8, 128), f32)],
        got,
        carry,
        *basis,
    )
    gram = jnp.sum(gram, axis=(1, 2))
    gram = jnp.sum(exchange(jnp.broadcast_to(gram[None, None], (devices, 1, pairs))), axis=(0, 1))
    factors = combination([gram[i] for i in range(pairs)])
    norm = 1.0 / (rows * columns)
    total = sum((amount * norm) * update for amount, update in zip(factors, updates))
    total = total.reshape(2, columns, spaces, inner, steps).transpose(4, 2, 0, 3, 1)
    total = exchange(total.reshape(devices, 2, inner, columns))
    return total.transpose(1, 2, 0, 3).reshape(2, 1, inner * devices, columns)


def solution(mesh):
    placed = (P(None, "space", None), P("space", None), P("space", None))
    return jax.shard_map(
        shards, mesh=mesh, in_specs=placed, out_specs=P(None, "tm", "space", None), check_vma=False
    )
```

```python
import functools
import math

import jax
import jax.numpy as jnp
import numpy as np
from jax import lax
from jax.experimental import pallas as pl
from jax.experimental.pallas import tpu as pltpu
from jax.sharding import PartitionSpec as P

ITERS = 4
tau = 400.0
alpha = 0.4
theta = alpha / (1.0 - alpha)
highest = lax.Precision.HIGHEST
AXES = ("tm", "space")
vmem = pl.BlockSpec(memory_space=pltpu.VMEM)


def with_halo(cells, axis, dim):
    count = lax.axis_size(axis)
    head = lax.slice_in_dim(cells, 0, 1, axis=dim)
    tail = lax.slice_in_dim(cells, cells.shape[dim] - 1, cells.shape[dim], axis=dim)
    return jnp.concatenate(
        [
            lax.ppermute(tail, axis, [(i, (i + 1) % count) for i in range(count)]),
            cells,
            lax.ppermute(head, axis, [((i + 1) % count, i) for i in range(count)]),
        ],
        axis=dim,
    )


def first_side(field, phase, absorb):
    padded = with_halo(field, "space", 1)
    curvature = (
        padded[:, 2:] + padded[:, :-2] + jnp.roll(field, 1, 2) + jnp.roll(field, -1, 2) - 4.0 * field
    )
    change_real = -tau * curvature[1] + phase * field[1] - absorb * field[0]
    change_imag = tau * curvature[0] - phase * field[0] - absorb * field[1]
    return field + 0.5 * jnp.stack([change_real, change_imag])


def factors_of(length):
    fine = 16
    index = np.arange(length)

    def pair(rows):
        angle = (rows[:, None] * index[None, :] % length) * (2.0 * math.pi / length)
        return np.cos(angle).astype(np.float32), np.sin(angle).astype(np.float32)

    return pair(np.arange(0, length, fine)) + pair(np.arange(fine))


def halves(value):
    high = value.astype(jnp.bfloat16)
    return high, (value - high.astype(jnp.float32)).astype(jnp.bfloat16)


def product(left, right):
    dot = functools.partial(jnp.dot, preferred_element_type=jnp.float32)
    return dot(left[0], right[0]) + (dot(left[0], right[1]) + dot(left[1], right[0]))


def table_kernel(chc_ref, chs_ref, clc_ref, cls_ref, cos_ref, sin_ref, ch_ref, cl_ref, sh_ref, sl_ref):
    fine = clc_ref.shape[0]
    low_cos, low_sin = clc_ref[...], cls_ref[...]
    for k in range(chc_ref.shape[0]):
        high_cos, high_sin = chc_ref[k : k + 1], chs_ref[k : k + 1]
        cosine = high_cos * low_cos - high_sin * low_sin
        sine = high_sin * low_cos + high_cos * low_sin
        rows = slice(k * fine, (k + 1) * fine)
        cos_ref[rows], sin_ref[rows] = cosine, sine
        ch_ref[rows], cl_ref[rows] = halves(cosine)
        sh_ref[rows], sl_ref[rows] = halves(sine)


def grid_kernel(
    steps, got_ref, ch_ref, cl_ref, sh_ref, sl_ref, lc_ref, ls_ref, phase_ref, absorb_ref, z_ref, out_ref
):
    devices, _, block, lanes = got_ref.shape
    size = devices * block
    cosine = (ch_ref[...], cl_ref[...])
    sine = (sh_ref[...], sl_ref[...])
    real = halves(got_ref[:, 0].reshape(size, lanes))
    imag = halves(got_ref[:, 1].reshape(size, lanes))
    mid_real = halves(product(cosine, real) - product(sine, imag))
    mid_imag = halves(product(sine, real) + product(cosine, imag))
    lane_cos, lane_sin = halves(lc_ref[0]), halves(ls_ref[0])
    back_cos, back_sin = halves(lc_ref[1]), halves(ls_ref[1])
    z_real = product(mid_real, back_cos) - product(mid_imag, back_sin)
    z_imag = product(mid_real, back_sin) + product(mid_imag, back_cos)
    z_ref[0] = z_real
    z_ref[1] = z_imag
    late = lax.broadcasted_iota(jnp.int32, (size, lanes), 1) % steps > 0
    sum_real = z_real + jnp.where(late, pltpu.roll(z_real, 1, 1), 0.0)
    sum_imag = z_imag + jnp.where(late, pltpu.roll(z_imag, 1, 1), 0.0)
    phase, absorb = phase_ref[...], absorb_ref[...]
    real = halves(absorb * sum_real - phase * sum_imag)
    imag = halves(absorb * sum_imag + phase * sum_real)
    mid_real = halves(product(real, lane_cos) + product(imag, lane_sin))
    mid_imag = halves(product(imag, lane_cos) - product(real, lane_sin))
    out_ref[:, 0] = (product(cosine, mid_real) + product(sine, mid_imag)).reshape(devices, block, lanes)
    out_ref[:, 1] = (product(cosine, mid_imag) - product(sine, mid_real)).reshape(devices, block, lanes)


def fourier(values, sign):
    count = len(values)
    if count == 1:
        return values
    even = fourier(values[0::2], sign)
    odd = fourier(values[1::2], sign)
    first, second = [], []
    for k in range(count // 2):
        angle = sign * 2.0 * math.pi * k / count
        cosine, sine = math.cos(angle), math.sin(angle)
        real, imag = odd[k]
        if k == 0:
            turned = (real, imag)
        elif 4 * k == count:
            turned = (-imag, real) if sign > 0 else (imag, -real)
        else:
            turned = (cosine * real - sine * imag, cosine * imag + sine * real)
        first.append((even[k][0] + turned[0], even[k][1] + turned[1]))
        second.append((even[k][0] - turned[0], even[k][1] - turned[1]))
    return first + second


def tile_of(block, lanes):
    return min(8, block), min(128, lanes)


def tiles(block, lanes, body):
    high, wide = tile_of(block, lanes)
    across = lanes // wide

    def tile(index, unused):
        row = pl.ds(pl.multiple_of(index // across * high, high), high)
        lane = pl.ds(pl.multiple_of(index % across * wide, wide), wide)
        body(row, lane)
        return 0

    lax.fori_loop(0, (block // high) * across, tile, 0)


def arrived(got_ref, carry_ref, row, lane):
    devices = got_ref.shape[0]
    values = [(got_ref[k, 0, row, lane], got_ref[k, 1, row, lane]) for k in range(devices)]
    values = fourier(values, -1)
    return [
        (values[k][0] + carry_ref[0, k, row, lane], values[k][1] + carry_ref[1, k, row, lane])
        for k in range(devices)
    ]


def mode_kernel(start, *refs):
    refs = list(refs)
    got_ref = refs.pop(0)
    carry_ref = None if start else refs.pop(0)
    real_ref, imag_ref = refs.pop(0), refs.pop(0)
    w_ref = None if start else refs.pop(0)
    z_ref, send_ref = refs
    devices, _, block, lanes = send_ref.shape

    def body(row, lane):
        if start:
            w = [(got_ref[0, k, row, lane], got_ref[1, k, row, lane]) for k in range(devices)]
        else:
            w = arrived(got_ref, carry_ref, row, lane)
        solved = []
        for k in range(devices):
            wr, wi = w[k]
            ratio_real, ratio_imag = real_ref[k, row, lane], imag_ref[k, row, lane]
            if not start:
                w_ref[0, k, row, lane] = wr
                w_ref[1, k, row, lane] = wi
            zr = wr * ratio_real + wi * ratio_imag
            zi = wi * ratio_real - wr * ratio_imag
            z_ref[0, k, row, lane] = zr
            z_ref[1, k, row, lane] = zi
            solved.append((zr, zi))
        solved = fourier(solved, 1)
        for k in range(devices):
            send_ref[k, 0, row, lane] = solved[k][0]
            send_ref[k, 1, row, lane] = solved[k][1]

    tiles(block, lanes, body)


def timed(ref, cosine, sine):
    _, devices, block, lanes = ref.shape
    real = halves(ref[0].reshape(devices * block, lanes))
    imag = halves(ref[1].reshape(devices * block, lanes))
    shape = (devices, block, lanes)
    return (
        (product(real, cosine) - product(imag, sine)).reshape(shape),
        (product(real, sine) + product(imag, cosine)).reshape(shape),
    )


def carry_kernel(w_ref, z_ref, q_ref, wrap_ref, time_ref, carry_ref, p_ref):
    p_ref[0], p_ref[1] = timed(w_ref, halves(time_ref[0]), halves(time_ref[1]))
    xr, xi = timed(z_ref, halves(wrap_ref[0]), halves(wrap_ref[1]))
    q = q_ref[...]
    carry_ref[0] = xr + q * xi - theta * w_ref[0]
    carry_ref[1] = xi - q * xr - theta * w_ref[1]


def gram_kernel(got_ref, carry_ref, time_ref, *refs):
    old_refs, gram_ref, w_ref = list(refs[:-2]), refs[-2], refs[-1]
    devices, _, block, lanes = got_ref.shape
    high, wide = tile_of(block, lanes)

    def place(row, lane):
        w = arrived(got_ref, carry_ref, row, lane)
        for k in range(devices):
            w_ref[0, k, row, lane] = w[k][0]
            w_ref[1, k, row, lane] = w[k][1]

    tiles(block, lanes, place)
    w_ref[0], w_ref[1] = timed(w_ref, halves(time_ref[0]), halves(time_ref[1]))
    gram_ref[...] = jnp.zeros_like(gram_ref)

    def body(row, lane):
        sums = {}
        for k in range(devices):
            vectors = [(r[0, k, row, lane], r[1, k, row, lane]) for r in old_refs + [w_ref]]
            at = 0
            for i in range(ITERS + 1):
                for j in range(i + 1):
                    term = vectors[i][0] * vectors[j][0] + vectors[i][1] * vectors[j][1]
                    sums[at] = term if k == 0 else sums[at] + term
                    at += 1
        for at in sums:
            gram_ref[at, 0:high, 0:wide] += sums[at]

    tiles(block, lanes, body)


def weigh_kernel(gram_ref, out_ref):
    factors = combination([gram_ref[i] for i in range(gram_ref.shape[0])])
    for i, factor in enumerate(factors):
        out_ref[i] = factor


def call(kernel, shapes, *args, scratch=()):
    out = [jax.ShapeDtypeStruct(shape, kind) for shape, kind in shapes]
    return pl.pallas_call(
        kernel,
        out_shape=out,
        in_specs=[vmem] * len(args),
        out_specs=[vmem] * len(out),
        scratch_shapes=scratch,
        compiler_params=pltpu.CompilerParams(vmem_limit_bytes=60 * 1024 * 1024),
    )(*args)


def least_squares(hessenberg, start):
    matrix = [list(line) for line in hessenberg]
    target = [start] + [jnp.zeros_like(start) for unused in range(ITERS)]
    cosines = []
    sines = []
    for column in range(ITERS):
        for row in range(column):
            upper = matrix[row][column]
            lower = matrix[row + 1][column]
            matrix[row][column] = cosines[row] * upper + sines[row] * lower
            matrix[row + 1][column] = -sines[row] * upper + cosines[row] * lower
        upper = matrix[column][column]
        lower = matrix[column + 1][column]
        radius = jnp.sqrt(upper * upper + lower * lower)
        cosines.append(upper / radius)
        sines.append(lower / radius)
        matrix[column][column] = radius
        target[column + 1] = -sines[column] * target[column]
        target[column] = cosines[column] * target[column]
    factors = [None] * ITERS
    for row in reversed(range(ITERS)):
        total = target[row]
        for other in range(row + 1, ITERS):
            total = total - matrix[row][other] * factors[other]
        factors[row] = total / matrix[row][row]
    return factors


def combination(gram):
    count = ITERS + 1
    entry = lambda i, j: gram[i * (i + 1) // 2 + j] if i >= j else gram[j * (j + 1) // 2 + i]
    norms = [jnp.sqrt(jnp.maximum(entry(i, i), 1e-30)) for i in range(count)]
    factor = [[None] * count for unused in range(count)]
    for j in range(count):
        for i in range(j, count):
            value = entry(i, j) / (norms[i] * norms[j])
            for k in range(j):
                value = value - factor[i][k] * factor[j][k]
            if i == j:
                factor[i][i] = jnp.sqrt(jnp.maximum(value, 1e-10))
            else:
                factor[i][j] = value / factor[j][j]
    zero = jnp.zeros_like(gram[0])
    upper = [[factor[j][i] * norms[j] if j >= i else zero for j in range(count)] for i in range(count)]
    matrix = [
        [(1.0 + theta) * upper[i][j] + upper[i][j + 1] for j in range(ITERS)] for i in range(count)
    ]
    return least_squares(matrix, norms[0] * factor[0][0])


def exchange(value):
    return lax.all_to_all(value, AXES, split_axis=0, concat_axis=0, tiled=True)


def shards(u_init, phase, absorb):
    steps, spaces = lax.axis_size("tm"), lax.axis_size("space")
    devices = steps * spaces
    columns = u_init.shape[2]
    rows = u_init.shape[1] * spaces
    block = columns // devices
    local = rows // devices
    lanes = local * steps
    inner = local // spaces
    f32 = jnp.float32
    me = lax.axis_index("tm") * spaces + lax.axis_index("space")
    half = ((columns, columns), jnp.bfloat16)
    full = ((columns, columns), f32)
    small = lax.optimization_barrier(tuple(jnp.asarray(x) for x in factors_of(columns)))
    cosine, sine, *table = call(table_kernel, [full] * 2 + [half] * 4, *small)
    if rows == columns:
        row_cos, row_sin = cosine, sine
    else:
        small = lax.optimization_barrier(tuple(jnp.asarray(x) for x in factors_of(rows)))
        full, half = ((rows, rows), f32), ((rows, rows), jnp.bfloat16)
        row_cos, row_sin = call(table_kernel, [full] * 2 + [half] * 4, *small)[:2]

    first = first_side(u_init, phase, absorb)
    pieces = jnp.concatenate([phase[None], absorb[None]]).reshape(2, inner, devices, columns)
    pieces = lax.dynamic_slice_in_dim(pieces, lax.axis_index("tm") * spaces, spaces, axis=2)
    pieces = lax.all_to_all(pieces, "space", split_axis=2, concat_axis=1, tiled=True)
    pieces = pieces.reshape(2, local, columns)
    spread = np.repeat(np.eye(local, dtype=np.float32), steps, axis=1)
    scale = 0.5 / (rows * columns * steps)
    wide_pieces = jnp.einsum("frq,rl->fql", pieces * scale, jnp.asarray(spread), precision=highest)

    mine = lax.axis_index("tm") * spaces * block
    need_cos = lax.dynamic_slice_in_dim(cosine, mine, spaces * block, axis=0)
    need_sin = lax.dynamic_slice_in_dim(sine, mine, spaces * block, axis=0)
    dot = functools.partial(jnp.einsum, precision=highest)
    column = jnp.stack(
        [
            dot("kq,pq->kp", need_cos, first[0]) + dot("kq,pq->kp", need_sin, first[1]),
            dot("kq,pq->kp", need_cos, first[1]) - dot("kq,pq->kp", need_sin, first[0]),
        ]
    )
    column = lax.all_to_all(column, "space", split_axis=1, concat_axis=2, tiled=True)
    side = jnp.stack(
        [
            dot("kp,pa->ka", column[0], row_cos) + dot("kp,pa->ka", column[1], row_sin),
            dot("kp,pa->ka", column[1], row_cos) - dot("kp,pa->ka", column[0], row_sin),
        ]
    )
    side = side.reshape(2, block, devices, local).transpose(0, 2, 1, 3)
    w = jnp.einsum("cmkr,rl->cmkl", side, jnp.asarray(spread), precision=highest)

    lane_index = jnp.arange(lanes) // steps
    mode_x = (lane_index[None, :] + local * jnp.arange(devices)[:, None]).astype(f32)
    mode_y = (me * block + jnp.arange(block)).astype(f32)
    symbol_x = 4.0 * jnp.sin(mode_x * (math.pi / rows)) ** 2
    symbol_y = 4.0 * jnp.sin(mode_y * (math.pi / columns)) ** 2
    q = 0.5 * tau * (symbol_x[:, None, :] + symbol_y[None, :, None])
    beta = alpha ** (1.0 / steps)
    turn = (jnp.arange(lanes) % steps).astype(f32) * (2.0 * math.pi / steps)
    cosine, sine = beta * jnp.cos(turn), beta * jnp.sin(turn)
    eigen_real = 1.0 - cosine + q * sine
    eigen_imag = sine + q * (1.0 + cosine)
    modulus = eigen_real * eigen_real + eigen_imag * eigen_imag
    coefs = (eigen_real / modulus, eigen_imag / modulus)

    place_of = jnp.arange(lanes)
    at, when = place_of // steps, place_of % steps
    angle = (at[None, :] * (me + devices * at[:, None])) % rows
    spin = (when[None, :] * when[:, None] % steps).astype(f32) * (2.0 * math.pi / steps)
    angle = angle.astype(f32) * (2.0 * math.pi / rows) + spin
    weight = jnp.float32(alpha) ** (when.astype(f32) / steps)
    lane_cos, lane_sin = jnp.cos(angle), jnp.sin(angle)
    up = weight[:, None]
    lane_cos = jnp.stack([lane_cos * up, (lane_cos / up).T])
    lane_sin = jnp.stack([lane_sin * up, (lane_sin / up).T])
    near = (at[:, None] == at[None, :]).astype(f32)
    back = near / weight[None, :]
    time_table = jnp.stack([back * jnp.cos(spin), back * jnp.sin(spin)])
    wrap_table = jnp.stack([near * cosine[:, None], near * -sine[:, None]]) / steps

    sent = ((devices, 2, block, lanes), f32)
    kept = ((2, devices, block, lanes), f32)
    field = ((2, columns, lanes), f32)
    z, send = call(functools.partial(mode_kernel, True), [kept, sent], w, *coefs)
    basis, updates = [], []
    for step in range(ITERS):
        carry, p = call(carry_kernel, [kept, kept], w, z, q, wrap_table, time_table)
        basis.append(p)
        update, out = call(
            functools.partial(grid_kernel, steps),
            [field, sent],
            exchange(send),
            *table,
            lane_cos,
            lane_sin,
            wide_pieces[0],
            wide_pieces[1],
        )
        updates.append(update)
        got = exchange(out)
        if step + 1 < ITERS:
            w, z, send = call(
                functools.partial(mode_kernel, False), [kept, kept, sent], got, carry, *coefs
            )
    pairs = (ITERS + 1) * (ITERS + 2) // 2
    (gram,) = call(
        gram_kernel,
        [((pairs, 8, 128), f32)],
        got,
        carry,
        time_table,
        *basis,
        scratch=[pltpu.VMEM(kept[0], f32)],
    )
    gram = jnp.sum(gram, axis=(1, 2))
    gram = jnp.sum(exchange(jnp.broadcast_to(gram[None, None], (devices, 1, pairs))), axis=(0, 1))
    gram = jnp.broadcast_to(gram[:, None, None], (pairs, 8, 128))
    (factors,) = call(weigh_kernel, [((ITERS, 8, 128), f32)], gram)
    factors = [factors[i, 0, 0] for i in range(ITERS)]
    norm = 1.0 / (rows * columns * steps)
    total = sum((amount * norm) * update for amount, update in zip(factors, updates))
    total = total.reshape(2, columns, spaces, inner, steps).transpose(4, 2, 0, 3, 1)
    total = exchange(total.reshape(devices, 2, inner, columns))
    return total.transpose(1, 2, 0, 3).reshape(2, 1, inner * devices, columns)


def solution(mesh):
    placed = (P(None, "space", None), P("space", None), P("space", None))
    return jax.shard_map(
        shards, mesh=mesh, in_specs=placed, out_specs=P(None, "tm", "space", None), check_vma=False
    )
```

```python
import functools
import math

import jax
import jax.numpy as jnp
import numpy as np
from jax import lax
from jax.experimental import pallas as pl
from jax.experimental.pallas import tpu as pltpu
from jax.sharding import PartitionSpec as P

ITERS = 4
tau = 400.0
alpha = 0.4
theta = alpha / (1.0 - alpha)
highest = lax.Precision.HIGH
AXES = ("tm", "space")
vmem = pl.BlockSpec(memory_space=pltpu.VMEM)


def with_halo(cells, axis, dim):
    count = lax.axis_size(axis)
    head = lax.slice_in_dim(cells, 0, 1, axis=dim)
    tail = lax.slice_in_dim(cells, cells.shape[dim] - 1, cells.shape[dim], axis=dim)
    return jnp.concatenate(
        [
            lax.ppermute(tail, axis, [(i, (i + 1) % count) for i in range(count)]),
            cells,
            lax.ppermute(head, axis, [((i + 1) % count, i) for i in range(count)]),
        ],
        axis=dim,
    )


def first_side(field, phase, absorb):
    padded = with_halo(field, "space", 1)
    curvature = (
        padded[:, 2:] + padded[:, :-2] + jnp.roll(field, 1, 2) + jnp.roll(field, -1, 2) - 4.0 * field
    )
    change_real = -tau * curvature[1] + phase * field[1] - absorb * field[0]
    change_imag = tau * curvature[0] - phase * field[0] - absorb * field[1]
    return field + 0.5 * jnp.stack([change_real, change_imag])


def factors_of(length):
    fine = 16
    index = lax.optimization_barrier(jnp.arange(length, dtype=jnp.int32))

    def pair(rows):
        angle = (rows[:, None] * index[None, :] % length).astype(jnp.float32) * (2.0 * math.pi / length)
        return jnp.cos(angle), jnp.sin(angle)

    return pair(index[::fine]) + pair(index[:fine])


def halves(value):
    high = value.astype(jnp.bfloat16)
    return high, (value - high.astype(jnp.float32)).astype(jnp.bfloat16)


def product(left, right):
    dot = functools.partial(jnp.dot, preferred_element_type=jnp.float32)
    return dot(left[0], right[0]) + (dot(left[0], right[1]) + dot(left[1], right[0]))


def table_kernel(chc_ref, chs_ref, clc_ref, cls_ref, cos_ref, sin_ref, ch_ref, cl_ref, sh_ref, sl_ref):
    fine = clc_ref.shape[0]
    low_cos, low_sin = clc_ref[...], cls_ref[...]
    for k in range(chc_ref.shape[0]):
        high_cos, high_sin = chc_ref[k : k + 1], chs_ref[k : k + 1]
        cosine = high_cos * low_cos - high_sin * low_sin
        sine = high_sin * low_cos + high_cos * low_sin
        rows = slice(k * fine, (k + 1) * fine)
        cos_ref[rows], sin_ref[rows] = cosine, sine
        ch_ref[rows], cl_ref[rows] = halves(cosine)
        sh_ref[rows], sl_ref[rows] = halves(sine)


def grid_kernel(
    steps, got_ref, ch_ref, cl_ref, sh_ref, sl_ref, lc_ref, ls_ref, phase_ref, absorb_ref, z_ref, out_ref,
    real_high, real_low, imag_high, imag_low,
):
    devices, _, block, lanes = got_ref.shape
    size = devices * block
    chunk = min(256, size)
    lane_cos, lane_sin = halves(lc_ref[0]), halves(ls_ref[0])
    back_cos, back_sin = halves(lc_ref[1]), halves(ls_ref[1])
    real = halves(got_ref[:, 0].reshape(size, lanes))
    imag = halves(got_ref[:, 1].reshape(size, lanes))
    late = lax.broadcasted_iota(jnp.int32, (chunk, lanes), 1) % steps > 0

    def rows_of(index):
        return pl.ds(pl.multiple_of(index * chunk, chunk), chunk)

    def inside(index, unused):
        rows = rows_of(index)
        cosine = (ch_ref[rows], cl_ref[rows])
        sine = (sh_ref[rows], sl_ref[rows])
        mid_real = halves(product(cosine, real) - product(sine, imag))
        mid_imag = halves(product(sine, real) + product(cosine, imag))
        z_real = product(mid_real, back_cos) - product(mid_imag, back_sin)
        z_imag = product(mid_real, back_sin) + product(mid_imag, back_cos)
        z_ref[0, rows] = z_real
        z_ref[1, rows] = z_imag
        sum_real = z_real + jnp.where(late, pltpu.roll(z_real, 1, 1), 0.0)
        sum_imag = z_imag + jnp.where(late, pltpu.roll(z_imag, 1, 1), 0.0)
        phase, absorb = phase_ref[rows], absorb_ref[rows]
        y_real = halves(absorb * sum_real - phase * sum_imag)
        y_imag = halves(absorb * sum_imag + phase * sum_real)
        high, low = halves(product(y_real, lane_cos) + product(y_imag, lane_sin))
        real_high[rows], real_low[rows] = high, low
        high, low = halves(product(y_imag, lane_cos) - product(y_real, lane_sin))
        imag_high[rows], imag_low[rows] = high, low
        return 0

    lax.fori_loop(0, size // chunk, inside, 0)
    mid_real = (real_high[...], real_low[...])
    mid_imag = (imag_high[...], imag_low[...])
    owners = chunk // block

    def outside(index, unused):
        rows = rows_of(index)
        to = pl.ds(index * owners, owners)
        cosine = (ch_ref[rows], cl_ref[rows])
        sine = (sh_ref[rows], sl_ref[rows])
        out_ref[to, 0] = (product(cosine, mid_real) + product(sine, mid_imag)).reshape(owners, block, lanes)
        out_ref[to, 1] = (product(cosine, mid_imag) - product(sine, mid_real)).reshape(owners, block, lanes)
        return 0

    lax.fori_loop(0, size // chunk, outside, 0)


def fourier(values, sign):
    count = len(values)
    if count == 1:
        return values
    even = fourier(values[0::2], sign)
    odd = fourier(values[1::2], sign)
    first, second = [], []
    for k in range(count // 2):
        angle = sign * 2.0 * math.pi * k / count
        cosine, sine = math.cos(angle), math.sin(angle)
        real, imag = odd[k]
        if k == 0:
            turned = (real, imag)
        elif 4 * k == count:
            turned = (-imag, real) if sign > 0 else (imag, -real)
        else:
            turned = (cosine * real - sine * imag, cosine * imag + sine * real)
        first.append((even[k][0] + turned[0], even[k][1] + turned[1]))
        second.append((even[k][0] - turned[0], even[k][1] - turned[1]))
    return first + second


def tile_of(block, lanes):
    return min(8, block), min(128, lanes)


def tiles(block, lanes, body):
    high, wide = tile_of(block, lanes)
    across = lanes // wide

    def tile(index, unused):
        row = pl.ds(pl.multiple_of(index // across * high, high), high)
        lane = pl.ds(pl.multiple_of(index % across * wide, wide), wide)
        body(row, lane)
        return 0

    lax.fori_loop(0, (block // high) * across, tile, 0)


def arrived(got_ref, carry_ref, row, lane):
    devices = got_ref.shape[0]
    values = [(got_ref[k, 0, row, lane], got_ref[k, 1, row, lane]) for k in range(devices)]
    values = fourier(values, -1)
    return [
        (values[k][0] + carry_ref[0, k, row, lane], values[k][1] + carry_ref[1, k, row, lane])
        for k in range(devices)
    ]


def mode_kernel(start, *refs):
    refs = list(refs)
    got_ref = refs.pop(0)
    carry_ref = None if start else refs.pop(0)
    real_ref, imag_ref = refs.pop(0), refs.pop(0)
    w_ref = None if start else refs.pop(0)
    z_ref, send_ref = refs
    devices, _, block, lanes = send_ref.shape

    def body(row, lane):
        if start:
            w = [(got_ref[0, k, row, lane], got_ref[1, k, row, lane]) for k in range(devices)]
        else:
            w = arrived(got_ref, carry_ref, row, lane)
        solved = []
        for k in range(devices):
            wr, wi = w[k]
            ratio_real, ratio_imag = real_ref[k, row, lane], imag_ref[k, row, lane]
            if not start:
                w_ref[0, k, row, lane] = wr
                w_ref[1, k, row, lane] = wi
            zr = wr * ratio_real + wi * ratio_imag
            zi = wi * ratio_real - wr * ratio_imag
            z_ref[0, k, row, lane] = zr
            z_ref[1, k, row, lane] = zi
            solved.append((zr, zi))
        solved = fourier(solved, 1)
        for k in range(devices):
            send_ref[k, 0, row, lane] = solved[k][0]
            send_ref[k, 1, row, lane] = solved[k][1]

    tiles(block, lanes, body)


def timed(ref, cosine, sine, write):
    _, devices, block, lanes = ref.shape
    owners = min(4, devices)

    def some(index, unused):
        to = pl.ds(index * owners, owners)
        real = halves(ref[0, to].reshape(owners * block, lanes))
        imag = halves(ref[1, to].reshape(owners * block, lanes))
        shape = (owners, block, lanes)
        write(
            to,
            (product(real, cosine) - product(imag, sine)).reshape(shape),
            (product(real, sine) + product(imag, cosine)).reshape(shape),
        )
        return 0

    lax.fori_loop(0, devices // owners, some, 0)


def carry_kernel(w_ref, z_ref, q_ref, wrap_ref, time_ref, carry_ref, p_ref):
    def put(to, real, imag):
        p_ref[0, to] = real
        p_ref[1, to] = imag

    def wrap(to, xr, xi):
        q = q_ref[to]
        carry_ref[0, to] = xr + q * xi - theta * w_ref[0, to]
        carry_ref[1, to] = xi - q * xr - theta * w_ref[1, to]

    timed(w_ref, halves(time_ref[0]), halves(time_ref[1]), put)
    timed(z_ref, halves(wrap_ref[0]), halves(wrap_ref[1]), wrap)


def gram_kernel(got_ref, carry_ref, time_ref, *refs):
    old_refs, gram_ref, w_ref = list(refs[:-2]), refs[-2], refs[-1]
    devices, _, block, lanes = got_ref.shape
    high, wide = tile_of(block, lanes)

    def place(row, lane):
        w = arrived(got_ref, carry_ref, row, lane)
        for k in range(devices):
            w_ref[0, k, row, lane] = w[k][0]
            w_ref[1, k, row, lane] = w[k][1]

    tiles(block, lanes, place)

    def put(to, real, imag):
        w_ref[0, to] = real
        w_ref[1, to] = imag

    timed(w_ref, halves(time_ref[0]), halves(time_ref[1]), put)
    gram_ref[...] = jnp.zeros_like(gram_ref)

    def body(row, lane):
        sums = {}
        for k in range(devices):
            vectors = [(r[0, k, row, lane], r[1, k, row, lane]) for r in old_refs + [w_ref]]
            at = 0
            for i in range(ITERS + 1):
                for j in range(i + 1):
                    term = vectors[i][0] * vectors[j][0] + vectors[i][1] * vectors[j][1]
                    sums[at] = term if k == 0 else sums[at] + term
                    at += 1
        for at in sums:
            gram_ref[at, 0:high, 0:wide] += sums[at]

    tiles(block, lanes, body)


def weigh_kernel(gram_ref, out_ref):
    factors = combination([gram_ref[i] for i in range(gram_ref.shape[0])])
    for i, factor in enumerate(factors):
        out_ref[i] = factor


def call(kernel, shapes, *args, scratch=()):
    out = [jax.ShapeDtypeStruct(shape, kind) for shape, kind in shapes]
    return pl.pallas_call(
        kernel,
        out_shape=out,
        in_specs=[vmem] * len(args),
        out_specs=[vmem] * len(out),
        scratch_shapes=scratch,
        compiler_params=pltpu.CompilerParams(vmem_limit_bytes=60 * 1024 * 1024),
    )(*args)


def least_squares(hessenberg, start):
    matrix = [list(line) for line in hessenberg]
    target = [start] + [jnp.zeros_like(start) for unused in range(ITERS)]
    cosines = []
    sines = []
    for column in range(ITERS):
        for row in range(column):
            upper = matrix[row][column]
            lower = matrix[row + 1][column]
            matrix[row][column] = cosines[row] * upper + sines[row] * lower
            matrix[row + 1][column] = -sines[row] * upper + cosines[row] * lower
        upper = matrix[column][column]
        lower = matrix[column + 1][column]
        radius = jnp.sqrt(upper * upper + lower * lower)
        cosines.append(upper / radius)
        sines.append(lower / radius)
        matrix[column][column] = radius
        target[column + 1] = -sines[column] * target[column]
        target[column] = cosines[column] * target[column]
    factors = [None] * ITERS
    for row in reversed(range(ITERS)):
        total = target[row]
        for other in range(row + 1, ITERS):
            total = total - matrix[row][other] * factors[other]
        factors[row] = total / matrix[row][row]
    return factors


def combination(gram):
    count = ITERS + 1
    entry = lambda i, j: gram[i * (i + 1) // 2 + j] if i >= j else gram[j * (j + 1) // 2 + i]
    norms = [jnp.sqrt(jnp.maximum(entry(i, i), 1e-30)) for i in range(count)]
    factor = [[None] * count for unused in range(count)]
    for j in range(count):
        for i in range(j, count):
            value = entry(i, j) / (norms[i] * norms[j])
            for k in range(j):
                value = value - factor[i][k] * factor[j][k]
            if i == j:
                factor[i][i] = jnp.sqrt(jnp.maximum(value, 1e-10))
            else:
                factor[i][j] = value / factor[j][j]
    zero = jnp.zeros_like(gram[0])
    upper = [[factor[j][i] * norms[j] if j >= i else zero for j in range(count)] for i in range(count)]
    matrix = [
        [(1.0 + theta) * upper[i][j] + upper[i][j + 1] for j in range(ITERS)] for i in range(count)
    ]
    return least_squares(matrix, norms[0] * factor[0][0])


def exchange(value):
    return lax.all_to_all(value, AXES, split_axis=0, concat_axis=0, tiled=True)


def shards(u_init, phase, absorb):
    steps, spaces = lax.axis_size("tm"), lax.axis_size("space")
    devices = steps * spaces
    columns = u_init.shape[2]
    rows = u_init.shape[1] * spaces
    block = columns // devices
    local = rows // devices
    lanes = local * steps
    inner = local // spaces
    f32 = jnp.float32
    me = lax.axis_index("tm") * spaces + lax.axis_index("space")
    half = ((columns, columns), jnp.bfloat16)
    full = ((columns, columns), f32)
    small = factors_of(columns)
    cosine, sine, *table = call(table_kernel, [full] * 2 + [half] * 4, *small)
    if rows == columns:
        row_cos, row_sin = cosine, sine
    else:
        small = factors_of(rows)
        full, half = ((rows, rows), f32), ((rows, rows), jnp.bfloat16)
        row_cos, row_sin = call(table_kernel, [full] * 2 + [half] * 4, *small)[:2]

    first = first_side(u_init, phase, absorb)
    pieces = jnp.concatenate([phase[None], absorb[None]]).reshape(2, inner, devices, columns)
    pieces = lax.dynamic_slice_in_dim(pieces, lax.axis_index("tm") * spaces, spaces, axis=2)
    pieces = lax.all_to_all(pieces, "space", split_axis=2, concat_axis=1, tiled=True)
    pieces = pieces.reshape(2, local, columns)
    spread = np.repeat(np.eye(local, dtype=np.float32), steps, axis=1)
    scale = 0.5 / (rows * columns * steps)
    wide_pieces = jnp.einsum("frq,rl->fql", pieces * scale, jnp.asarray(spread), precision=highest)

    mine = lax.axis_index("tm") * spaces * block
    need_cos = lax.dynamic_slice_in_dim(cosine, mine, spaces * block, axis=0)
    need_sin = lax.dynamic_slice_in_dim(sine, mine, spaces * block, axis=0)
    dot = functools.partial(jnp.einsum, precision=highest)
    column = jnp.stack(
        [
            dot("kq,pq->kp", need_cos, first[0]) + dot("kq,pq->kp", need_sin, first[1]),
            dot("kq,pq->kp", need_cos, first[1]) - dot("kq,pq->kp", need_sin, first[0]),
        ]
    )
    column = lax.all_to_all(column, "space", split_axis=1, concat_axis=2, tiled=True)
    side = jnp.stack(
        [
            dot("kp,pa->ka", column[0], row_cos) + dot("kp,pa->ka", column[1], row_sin),
            dot("kp,pa->ka", column[1], row_cos) - dot("kp,pa->ka", column[0], row_sin),
        ]
    )
    side = side.reshape(2, block, devices, local).transpose(0, 2, 1, 3)
    w = jnp.einsum("cmkr,rl->cmkl", side, jnp.asarray(spread), precision=highest)

    lane_index = jnp.arange(lanes) // steps
    mode_x = (lane_index[None, :] + local * jnp.arange(devices)[:, None]).astype(f32)
    mode_y = (me * block + jnp.arange(block)).astype(f32)
    symbol_x = 4.0 * jnp.sin(mode_x * (math.pi / rows)) ** 2
    symbol_y = 4.0 * jnp.sin(mode_y * (math.pi / columns)) ** 2
    q = 0.5 * tau * (symbol_x[:, None, :] + symbol_y[None, :, None])
    beta = alpha ** (1.0 / steps)
    turn = (jnp.arange(lanes) % steps).astype(f32) * (2.0 * math.pi / steps)
    cosine, sine = beta * jnp.cos(turn), beta * jnp.sin(turn)
    eigen_real = 1.0 - cosine + q * sine
    eigen_imag = sine + q * (1.0 + cosine)
    modulus = eigen_real * eigen_real + eigen_imag * eigen_imag
    coefs = (eigen_real / modulus, eigen_imag / modulus)

    place_of = jnp.arange(lanes)
    at, when = place_of // steps, place_of % steps
    angle = (at[None, :] * (me + devices * at[:, None])) % rows
    spin = (when[None, :] * when[:, None] % steps).astype(f32) * (2.0 * math.pi / steps)
    angle = angle.astype(f32) * (2.0 * math.pi / rows) + spin
    weight = jnp.float32(alpha) ** (when.astype(f32) / steps)
    lane_cos, lane_sin = jnp.cos(angle), jnp.sin(angle)
    up = weight[:, None]
    lane_cos = jnp.stack([lane_cos * up, (lane_cos / up).T])
    lane_sin = jnp.stack([lane_sin * up, (lane_sin / up).T])
    near = (at[:, None] == at[None, :]).astype(f32)
    back = near / weight[None, :]
    time_table = jnp.stack([back * jnp.cos(spin), back * jnp.sin(spin)])
    wrap_table = jnp.stack([near * cosine[:, None], near * -sine[:, None]]) / steps

    sent = ((devices, 2, block, lanes), f32)
    kept = ((2, devices, block, lanes), f32)
    field = ((2, columns, lanes), f32)
    z, send = call(functools.partial(mode_kernel, True), [kept, sent], w, *coefs)
    basis, updates = [], []
    for step in range(ITERS):
        carry, p = call(carry_kernel, [kept, kept], w, z, q, wrap_table, time_table)
        basis.append(p)
        update, out = call(
            functools.partial(grid_kernel, steps),
            [field, sent],
            exchange(send),
            *table,
            lane_cos,
            lane_sin,
            wide_pieces[0],
            wide_pieces[1],
            scratch=[pltpu.VMEM((columns, lanes), jnp.bfloat16)] * 4,
        )
        updates.append(update)
        got = exchange(out)
        if step + 1 < ITERS:
            w, z, send = call(
                functools.partial(mode_kernel, False), [kept, kept, sent], got, carry, *coefs
            )
    pairs = (ITERS + 1) * (ITERS + 2) // 2
    (gram,) = call(
        gram_kernel,
        [((pairs, 8, 128), f32)],
        got,
        carry,
        time_table,
        *basis,
        scratch=[pltpu.VMEM(kept[0], f32)],
    )
    gram = jnp.sum(gram, axis=(1, 2))
    gram = jnp.sum(exchange(jnp.broadcast_to(gram[None, None], (devices, 1, pairs))), axis=(0, 1))
    gram = jnp.broadcast_to(gram[:, None, None], (pairs, 8, 128))
    (factors,) = call(weigh_kernel, [((ITERS, 8, 128), f32)], gram)
    factors = [factors[i, 0, 0] for i in range(ITERS)]
    norm = 1.0 / (rows * columns * steps)
    total = sum((amount * norm) * update for amount, update in zip(factors, updates))
    total = total.reshape(2, columns, spaces, inner, steps).transpose(4, 2, 0, 3, 1)
    total = exchange(total.reshape(devices, 2, inner, columns))
    return total.transpose(1, 2, 0, 3).reshape(2, 1, inner * devices, columns)


def solution(mesh):
    placed = (P(None, "space", None), P("space", None), P("space", None))
    return jax.shard_map(
        shards, mesh=mesh, in_specs=placed, out_specs=P(None, "tm", "space", None), check_vma=False
    )
```
